256 devices in a mesh: half: 2 (over core), prow: 16 (over z, x_hi), pcol: 8 (over x_lo, y).
Axes of the slice: x: 4 (x_hi: 2, x_lo: 2; x = x_hi * 2 + x_lo), y: 4, z: 8, core: 2. Of those that a mesh axis runs over, the one named last changes fastest.
Arguments:
- child_update: float32 [2, 8192, 8192], P('half', 'prow', 'pcol'), may hold values from -6 to 6, as said below
- child_panel: float32 [2, 8192, 1024], P('half', 'prow'), may hold values from -3 to 3
- root_front: float32 [12288, 12288], P('prow', ('half', 'pcol')), may hold values from -29 to 6144, as said below
- index_map: int32 [2, 64], replicated, may hold values from 0 to 95, as said below
Outputs:
- root_next: float32 [12288, 12288], P('prow', ('half', 'pcol'))
The draws below stay inside these ranges and needn't reach their ends.
Inputs may be any that keep to these rules, and one draw needn't show every extreme that they name: `child_update`: each child's matrix is symmetric. `root_front`: Symmetric. `index_map`: for each child the entries are distinct, and child 0 names the blocks 0 to 1. Of the 8 blocks of one process row of both children (blocks p * 4 on), at most 1 share one root process row v // 6; of the 8 blocks of one child process column (blocks q * 8 on), at most 1 share one root column group v // 6; both bounds are reached.
All inputs are finite; a program needn't handle non-finite values.
Results may differ from the reference program's by a relative error of at most 0.00016.
Values sent between devices are 32-bit elements; how exact they have to be, the bound alone decides.
A program may use at most 128 MiB of HBM per device.

```python
import jax
import jax.numpy as jnp
from jax import lax

BLK = 128
MBLK = 64
RBLK = 96
RPB = 2
PANEL = 1024
CHILD = 8192
NR = 12288
RP = 256
N_PROW = 16
N_PCOL = 8


def draw_child_update(key, part):
    values = jax.random.truncated_normal(key, -4.0, 4.0, (2, CHILD, CHILD), jnp.float32)
    return (values + jnp.swapaxes(values, 1, 2)) * 0.7071


def draw_root_front(key, part):
    key_base, key_off, key_diag = jax.random.split(key, 3)
    values = jax.random.truncated_normal(key_base, -4.0, 4.0, (NR, NR), jnp.float32)
    values = (values + values.T) * 0.7071
    values = values.at[RP:, :RP].multiply(5.0).at[:RP, RP:].multiply(5.0)
    coupling = jax.random.uniform(key_off, (RP, RP), jnp.float32, -1.0, 1.0)
    coupling = 0.5 * (coupling + coupling.T)
    diagonal = jax.random.uniform(key_diag, (RP,), jnp.float32, 16.0 * RP, 24.0 * RP)
    identity = jnp.eye(RP, dtype=jnp.float32)
    pivot_block = coupling * (1.0 - identity) + identity * diagonal[None, :]
    return values.at[:RP, :RP].set(pivot_block)


def draw_index_map(key, part):
    child_rows = MBLK // N_PROW
    root_rows = RBLK // N_PROW
    width = N_PROW // (2 * N_PCOL)
    key_off, key_group, key_item, key_slot = jax.random.split(key, 4)
    offset = jax.random.randint(key_off, (), 0, N_PROW)
    group_perm = jax.random.permutation(key_group, 2 * N_PCOL).astype(jnp.int32)
    item_perm = jax.vmap(lambda subkey: jax.random.permutation(subkey, child_rows))(jax.random.split(key_item, 2 * N_PROW)).reshape(2, N_PROW, child_rows)
    blocks = jnp.arange(N_PROW, dtype=jnp.int32)[None, :, None] * child_rows + item_perm.astype(jnp.int32)
    child_shift = jnp.arange(2, dtype=jnp.int32)[:, None, None] * child_rows
    base = (blocks + child_shift + offset) % N_PROW
    owner = (jnp.take(group_perm, base // width) * width + base % width).reshape(2, MBLK).astype(jnp.int32)
    onehot = (owner[:, :, None] == jnp.arange(N_PROW, dtype=jnp.int32)[None, None, :]).astype(jnp.int32)
    ranks = jnp.sum((jnp.cumsum(onehot, axis=1) - 1) * onehot, axis=2)
    slot_orders = jax.vmap(lambda subkey: jax.random.permutation(subkey, root_rows))(jax.random.split(key_slot, 2 * N_PROW)).reshape(2, N_PROW, root_rows).astype(jnp.int32)
    forced = jnp.zeros((2, N_PROW, root_rows), jnp.int32)
    forced = forced.at[0, 0, :RPB].set(1).at[0, N_PROW - 1, root_rows - 1].set(1)
    priority = slot_orders - forced * root_rows
    slot_table = jnp.argsort(priority, axis=2).astype(jnp.int32).reshape(2, N_PROW * root_rows)
    slots = jnp.take_along_axis(slot_table, owner * root_rows + ranks, axis=1)
    return (owner * root_rows + slots).astype(jnp.int32)


def block_levels(key, extent, shards, least, largest):
    factor_of = 1.0
    for axis_at, parts in shards:
        heights = jax.random.uniform(jax.random.fold_in(jax.random.fold_in(key, 6), axis_at), (parts,), jnp.float32, least / len(shards), largest / len(shards))
        factor_of = factor_of * jnp.repeat(jnp.exp(heights), extent[axis_at] // parts).reshape((-1,) + (1,) * (len(extent) - 1 - axis_at))
    return factor_of


def bell_draw(key, dims, spread, reach, pieces=(), kind=jnp.bfloat16):
    array = spread * jax.random.normal(key, dims, jnp.float32)
    if pieces:
        array = array * block_levels(key, dims, pieces, -0.22, 0.18)
    return jnp.clip(array, -reach, reach).astype(kind)


def setup_inputs(seed: int = 0) -> dict:
    key_of = jax.random.split(jax.random.key(seed), 5)
    return {
        "child_update": draw_child_update(jax.random.fold_in(key_of[4], 71), 0),
        "child_panel": bell_draw(key_of[1], (2, CHILD, PANEL), 0.2, 3.0, ((0, 2), (1, 16)), jnp.float32),
        "root_front": draw_root_front(jax.random.fold_in(key_of[4], 71), 0),
        "index_map": draw_index_map(jax.random.fold_in(key_of[4], 71), 0),
    }


def reference(child_update, child_panel, root_front, index_map):
    root_blocks = root_front.reshape(RBLK, BLK, RBLK, BLK)
    for child_index in range(2):
        panel_part = child_panel[child_index]
        product = lax.dot_general(panel_part.astype(jnp.float32), panel_part.astype(jnp.float32), (((1,), (1,)), ((), ())), precision=lax.Precision.HIGHEST, preferred_element_type=jnp.float32)
        schur_part = child_update[child_index] - product
        child_tiles = schur_part.reshape(MBLK, BLK, MBLK, BLK).transpose(0, 2, 1, 3)
        targets = index_map[child_index].astype(jnp.int32)
        root_blocks = root_blocks.at[targets[:, None], :, targets[None, :], :].add(child_tiles)
    assembled = root_blocks.reshape(NR, NR)
    factor = jnp.linalg.cholesky(assembled[:RP, :RP])
    lower = lax.linalg.triangular_solve(factor, assembled[RP:, :RP], left_side=False, lower=True, transpose_a=True)
    update = lax.dot_general(lower.astype(jnp.float32), lower.astype(jnp.float32), (((1,), (1,)), ((), ())), precision=lax.Precision.HIGHEST, preferred_element_type=jnp.float32)
    trailing = assembled[RP:, RP:] - update
    panel_cols = jnp.concatenate([factor, lower], axis=0)
    right_side = jnp.concatenate([assembled[:RP, RP:], trailing], axis=0)
    return jnp.concatenate([panel_cols, right_side], axis=1)
```

```python
import functools

import jax
import jax.numpy as jnp
from jax import lax
from jax.experimental import pallas as pl
from jax.experimental.pallas import tpu as pltpu
from jax.sharding import PartitionSpec as P

BLK = 128
RP = 256
HALF = BLK // 2
NZ = 8
CHUNKS = 32
MESH = pl.DeviceIdType.MESH
ANY = pl.BlockSpec(memory_space=pl.ANY)


def position():
    return lax.axis_index("half"), lax.axis_index("prow"), lax.axis_index("pcol")


def greet(devices):
    barrier = pltpu.get_barrier_semaphore()
    for device in devices:
        pl.semaphore_signal(barrier, inc=1, device_id=device, device_id_type=MESH)
    pl.semaphore_wait(barrier, len(devices))


def spread_kernel(panel, out, local_sem, up_send, up_recv, down_send, down_recv, side_send):
    child, prow, pcol = position()
    z, x = prow // 2, prow % 2
    other_x = 1 - x
    up = (child, ((z + 1) % NZ) * 2 + x, pcol)
    down = (child, ((z + NZ - 1) % NZ) * 2 + x, pcol)
    side = (child, z * 2 + other_x, (pcol + 4) % 8)
    greet((up, down, side))
    rows = panel.shape[0] // CHUNKS
    above = (z + NZ - pcol) % NZ
    below = (pcol + NZ - z) % NZ
    from_side = z == (pcol + 4) % 8

    def piece(index):
        return pl.ds(pl.multiple_of(index * rows, rows), rows)

    def up_copy(index, source):
        return pltpu.make_async_remote_copy(
            source, out.at[x, piece(index)], up_send.at[index], up_recv.at[index],
            device_id=up, device_id_type=MESH)

    def down_copy(index):
        there = out.at[other_x, piece(index)]
        return pltpu.make_async_remote_copy(
            there, there, down_send.at[index], down_recv.at[index],
            device_id=down, device_id_type=MESH)

    def side_copy(index):
        return pltpu.make_async_remote_copy(
            panel.at[piece(index)], out.at[x, piece(index)], side_send.at[index],
            down_recv.at[index], device_id=side, device_id_type=MESH)

    own = pltpu.make_async_copy(panel, out.at[x], local_sem)

    @pl.when(from_side)
    def _():
        @pl.loop(0, CHUNKS)
        def _(index):
            side_copy(index).start()

    @pl.when(above == 0)
    def _():
        @pl.loop(0, CHUNKS)
        def _(index):
            up_copy(index, panel.at[piece(index)]).start()

        own.start()

    up_lag = (3 * above) // 2
    down_lag = (3 * below) // 2 + 1

    @pl.loop(0, CHUNKS + 12)
    def _(step):
        up_index = step - up_lag
        down_index = step - down_lag

        @pl.when((above > 0) & (up_index >= 0) & (up_index < CHUNKS))
        def _():
            copy = up_copy(up_index, out.at[x, piece(up_index)])
            copy.wait_recv()

            @pl.when(above < NZ - 1)
            def _():
                copy.start()

        @pl.when((down_index >= 0) & (down_index < CHUNKS))
        def _():
            copy = down_copy(down_index)
            copy.wait_recv()

            @pl.when(below < NZ - 1)
            def _():
                copy.start()

    @pl.when(above < NZ - 1)
    def _():
        @pl.loop(0, CHUNKS)
        def _(index):
            up_copy(index, panel.at[piece(index)]).wait_send()

    @pl.when(below < NZ - 1)
    def _():
        @pl.loop(0, CHUNKS)
        def _(index):
            down_copy(index).wait_send()

    @pl.when(from_side)
    def _():
        @pl.loop(0, CHUNKS)
        def _(index):
            side_copy(index).wait_send()

    @pl.when(above == 0)
    def _():
        own.wait()


def spread(panel):
    rows, cols = panel.shape
    sems = pltpu.SemaphoreType.DMA((CHUNKS,))
    return pl.pallas_call(
        spread_kernel,
        out_shape=jax.ShapeDtypeStruct((2, rows, cols), jnp.float32),
        in_specs=[ANY],
        out_specs=ANY,
        scratch_shapes=[pltpu.SemaphoreType.DMA] + [sems] * 5,
        compiler_params=pltpu.CompilerParams(collective_id=0, has_side_effects=True),
    )(panel)


def split(value):
    high = value.astype(jnp.bfloat16)
    return high, (value - high.astype(jnp.float32)).astype(jnp.bfloat16)


def dot3(left, right, dims):
    dot = functools.partial(
        lax.dot_general, dimension_numbers=(dims, ((), ())), preferred_element_type=jnp.float32)
    return dot(left[0], right[0]) + (dot(left[0], right[1]) + dot(left[1], right[0]))


def schur_kernel(panel, columns, update, out, high, low):
    @pl.when(pl.program_id(0) == 0)
    def _():
        high[...], low[...] = split(panel[...])

    product = dot3((high[...], low[...]), split(columns[...]), ((1,), (1,)))
    value = update[...] - product
    for block in range(out.shape[1]):
        for half in range(2):
            start = block * BLK + half * HALF
            out[half, block] = value[start : start + HALF]


def schur(panel, columns, update):
    rows, depth = panel.shape
    tile = 256
    width = update.shape[1]
    blocks = rows // BLK
    return pl.pallas_call(
        schur_kernel,
        out_shape=jax.ShapeDtypeStruct((2, blocks, HALF, width), jnp.float32),
        grid=(width // tile,),
        in_specs=[
            pl.BlockSpec((rows, depth), lambda n: (0, 0)),
            pl.BlockSpec((tile, depth), lambda n: (n, 0)),
            pl.BlockSpec((rows, tile), lambda n: (0, n)),
        ],
        out_specs=pl.BlockSpec((2, blocks, HALF, tile), lambda n: (0, 0, 0, n)),
        scratch_shapes=[pltpu.VMEM((rows, depth), jnp.bfloat16)] * 2,
    )(panel, columns, update)


def pick_kernel(index, source, out):
    out[...] = source[...]


def pick(index, source, count):
    block = (1,) + source.shape[1:]
    return pl.pallas_call(
        pick_kernel,
        out_shape=jax.ShapeDtypeStruct((count,) + source.shape[1:], jnp.float32),
        grid_spec=pltpu.PrefetchScalarGridSpec(
            num_scalar_prefetch=1,
            grid=(count,),
            in_specs=[pl.BlockSpec(block, lambda n, index: (index[n], 0, 0))],
            out_specs=pl.BlockSpec(block, lambda n, index: (n, 0, 0)),
        ),
    )(index, source)


def deal_kernel(rows, cols, arrived, out):
    child = pl.program_id(0)
    for group in range(out.shape[0]):
        start = pl.multiple_of(cols[child, group] * BLK, BLK)
        out[group, 0, 0] = arrived[0, :, pl.ds(start, BLK)]


def deal(rows, cols, arrived, groups, slots):
    width = arrived.shape[2]
    return pl.pallas_call(
        deal_kernel,
        out_shape=jax.ShapeDtypeStruct((groups, 2, slots, HALF, BLK), jnp.float32),
        grid_spec=pltpu.PrefetchScalarGridSpec(
            num_scalar_prefetch=2,
            grid=(2, slots),
            in_specs=[
                pl.BlockSpec((1, HALF, width), lambda c, i, rows, cols: (rows[c, i], 0, 0))],
            out_specs=pl.BlockSpec(
                (groups, 1, 1, HALF, BLK), lambda c, i, rows, cols: (0, c, i, 0, 0)),
        ),
    )(rows, cols, arrived)


def extend_kernel(source, row_there, col_there, root, *refs):
    parts, out = refs[:-1], refs[-1]
    column = pl.program_id(0)
    for slot in range(out.shape[0] // BLK):
        for half in range(2):
            rows = pl.ds(slot * BLK + half * HALF, HALF)
            value = root[rows, :]
            for child in range(2):
                there = row_there[child, slot] * col_there[child, column] > 0
                part = parts[child * 2 + half][0, 0, slot]
                value = value + jnp.where(there, part, 0.0)
            out[rows, :] = value


def extend(source, row_there, col_there, root, incoming):
    rows, cols = root.shape
    slots = cols // BLK
    groups = incoming.shape[0] // 2

    def part(child, half):
        return pl.BlockSpec(
            (1, 1, rows // BLK, HALF, BLK),
            lambda j, source, *_: (half * groups + source[child, j], child, 0, 0, 0))

    column = pl.BlockSpec((rows, BLK), lambda j, *_: (0, j))
    return pl.pallas_call(
        extend_kernel,
        out_shape=jax.ShapeDtypeStruct(root.shape, jnp.float32),
        grid_spec=pltpu.PrefetchScalarGridSpec(
            num_scalar_prefetch=3,
            grid=(slots,),
            in_specs=[column] + [part(c, h) for c in range(2) for h in range(2)],
            out_specs=column,
        ),
    )(source, row_there, col_there, root, *[incoming] * 4)


def share_kernel(row_raw, col_raw, row_out, col_out, pivot_out, local_sem, *sems):
    (row_in, row_cast, row_recv, row_send, col_in, col_cast, col_recv, col_send,
     pivot_in, pivot_cast, pivot_mid, pivot_down, pivot_recv, pivot_send) = sems
    half, prow, pcol = position()
    count = 16
    group = half * 8 + pcol

    def in_row(k):
        return (k // 8, prow, k % 8)

    def in_col(k):
        return (half, k, pcol)

    greet([in_row((group + k) % count) for k in range(1, count)]
          + [in_col((prow + k) % count) for k in range(1, count)])
    row_piece, col_piece, pivot_piece = row_out.shape[1], col_out.shape[1], pivot_out.shape[1]
    pivot_owner = (group == 0) & (prow == 0)

    def cut(ref, k, size):
        return ref.at[pl.ds(pl.multiple_of(k * size, size), size)]

    def remote(source, target, send, recv, device):
        return pltpu.make_async_remote_copy(
            source, target, send, recv, device_id=device, device_id_type=MESH)

    def others(me, body):
        @pl.loop(1, count)
        def _(step):
            body((me + step) % count)

    def pivot_first(k):
        return remote(cut(row_raw, k, pivot_piece), pivot_out.at[k], pivot_cast.at[k],
                      pivot_in, in_row(k))

    def pivot_second(k):
        return remote(pivot_out.at[group], pivot_out.at[group], pivot_down.at[k],
                      pivot_mid, in_col(k))

    def pivot_third(k):
        return remote(pivot_out.at[group], pivot_out.at[group], pivot_send.at[k],
                      pivot_recv.at[group], in_row(k))

    def row_first(k):
        return remote(cut(row_raw, k, row_piece), row_out.at[k], row_cast.at[k], row_in, in_row(k))

    def row_second(k):
        return remote(row_out.at[group], row_out.at[group], row_send.at[k], row_recv.at[group],
                      in_row(k))

    def col_first(k):
        return remote(cut(col_raw, k, col_piece), col_out.at[k], col_cast.at[k], col_in, in_col(k))

    def col_second(k):
        return remote(col_out.at[prow], col_out.at[prow], col_send.at[k], col_recv.at[prow],
                      in_col(k))

    @pl.when(pivot_owner)
    def _():
        others(group, lambda k: pivot_first(k).start())

    @pl.when(group == 0)
    def _():
        others(group, lambda k: row_first(k).start())

    @pl.when(prow == 0)
    def _():
        others(prow, lambda k: col_first(k).start())

    def keep(source, target, size):
        @pl.loop(0, count)
        def _(k):
            pltpu.make_async_copy(cut(source, k, size), target.at[k], local_sem).start()
        @pl.loop(0, count)
        def _(k):
            pltpu.make_async_copy(cut(source, k, size), target.at[k], local_sem).wait()

    @pl.when(pivot_owner)
    def _():
        keep(row_raw, pivot_out, pivot_piece)

    @pl.when(prow == 0)
    def _():
        @pl.when(group > 0)
        def _():
            pivot_first(group).wait_recv()

        others(prow, lambda k: pivot_second(k).start())

    @pl.when(group == 0)
    def _():
        keep(row_raw, row_out, row_piece)

    @pl.when(prow == 0)
    def _():
        keep(col_raw, col_out, col_piece)

    @pl.when(group > 0)
    def _():
        row_first(group).wait_recv()

    def skip_first(k, body):
        @pl.when(k > 0)
        def _():
            body()

    others(group, lambda k: skip_first(k, lambda: row_second(k).start()))

    @pl.when(prow > 0)
    def _():
        pivot_second(prow).wait_recv()

    def skip_owner(k, body):
        @pl.when((prow > 0) | (k > 0))
        def _():
            body()

    others(group, lambda k: skip_owner(k, lambda: pivot_third(k).start()))

    @pl.when(prow > 0)
    def _():
        col_first(prow).wait_recv()

    others(prow, lambda k: skip_first(k, lambda: col_second(k).start()))

    def arrive(target, recv, k):
        remote(target.at[k], target.at[k], local_sem, recv.at[k], in_row(k)).wait_recv()

    @pl.when(jnp.logical_not(pivot_owner))
    def _():
        others(group, lambda k: arrive(pivot_out, pivot_recv, k))

    @pl.when(group > 0)
    def _():
        others(group, lambda k: arrive(row_out, row_recv, k))

    @pl.when(prow > 0)
    def _():
        others(prow, lambda k: arrive(col_out, col_recv, k))

    @pl.when(pivot_owner)
    def _():
        others(group, lambda k: pivot_first(k).wait_send())

    @pl.when(group == 0)
    def _():
        others(group, lambda k: row_first(k).wait_send())

    @pl.when(prow == 0)
    def _():
        others(prow, lambda k: col_first(k).wait_send())
        others(prow, lambda k: pivot_second(k).wait_send())

    others(group, lambda k: skip_first(k, lambda: row_second(k).wait_send()))
    others(group, lambda k: skip_owner(k, lambda: pivot_third(k).wait_send()))
    others(prow, lambda k: skip_first(k, lambda: col_second(k).wait_send()))


def share(row_raw, col_raw):
    count = 16
    one, many = pltpu.SemaphoreType.DMA, pltpu.SemaphoreType.DMA((count,))
    rows, cols = row_raw.shape[0], col_raw.shape[1]
    row_out, col_out, pivot = pl.pallas_call(
        share_kernel,
        out_shape=(
            jax.ShapeDtypeStruct((count, rows // count, RP), jnp.float32),
            jax.ShapeDtypeStruct((count, RP // count, cols), jnp.float32),
            jax.ShapeDtypeStruct((count, RP // count, RP), jnp.float32),
        ),
        in_specs=[ANY, ANY],
        out_specs=(ANY, ANY, ANY),
        scratch_shapes=[one, one, many, many, many, one, many, many, many,
                        one, many, one, many, many, many],
        compiler_params=pltpu.CompilerParams(collective_id=1, has_side_effects=True),
    )(row_raw, col_raw)
    return row_out.reshape(rows, RP), col_out.reshape(RP, cols), pivot.reshape(RP, RP)


def find(labels, wanted, values):
    hit = labels[..., None, :] == wanted[:, None]
    return jnp.sum(jnp.where(hit, values, 0), axis=-1).astype(jnp.int32), jnp.any(hit, axis=-1)


def shards(child_update, child_panel, root_front, index_map):
    rows_dev, cols_dev = child_update.shape[1:]
    root_rows, root_cols = root_front.shape
    row_count, col_count, groups = 16, 8, 16
    row_index = lax.axis_index("prow")
    col_index = lax.axis_index("pcol")
    group_index = lax.axis_index(("half", "pcol"))
    row_slots, col_slots = root_rows // BLK, root_cols // BLK
    child_blocks, col_blocks = rows_dev // BLK, cols_dev // BLK
    blocks = jnp.arange(index_map.shape[1], dtype=jnp.int32)
    everyone = jnp.arange(row_count, dtype=jnp.int32)

    own_rows = lax.dynamic_slice_in_dim(index_map, row_index * child_blocks, child_blocks, 1)
    leaves, _ = find(own_rows.reshape(-1) // row_slots, everyone,
                     jnp.arange(2 * child_blocks, dtype=jnp.int32))
    row_source, row_there = find(
        index_map, row_index * row_slots + jnp.arange(row_slots, dtype=jnp.int32),
        blocks // child_blocks)
    own_cols = lax.dynamic_slice_in_dim(index_map, col_index * col_blocks, col_blocks, 1)
    col_leaves, _ = find(own_cols // col_slots, everyone, jnp.arange(col_blocks, dtype=jnp.int32))
    col_source, col_there = find(
        index_map, group_index * col_slots + jnp.arange(col_slots, dtype=jnp.int32),
        blocks // col_blocks)

    own_panel = child_panel[0]
    columns = spread(own_panel).reshape(cols_dev, -1)
    part = schur(own_panel, columns, child_update[0])
    both = lax.all_to_all(part, "half", split_axis=0, concat_axis=0, tiled=True)
    outgoing = pick(leaves, both.reshape(2 * child_blocks, HALF, cols_dev), row_count)
    arrived = lax.all_to_all(outgoing, "prow", split_axis=0, concat_axis=0, tiled=True)
    dealt = deal(row_source, col_leaves, arrived, groups, row_slots)
    incoming = lax.all_to_all(dealt, ("half", "pcol"), split_axis=0, concat_axis=0, tiled=True)
    assembled = extend(col_source, row_there.astype(jnp.int32), col_there.astype(jnp.int32),
                       root_front, incoming)

    high = lax.Precision.HIGH
    row_raw, col_raw, pivot = share(assembled[:, :RP], assembled[:RP, :])
    factor = jnp.linalg.cholesky(pivot)
    inverse = lax.linalg.triangular_solve(
        factor, jnp.eye(RP, dtype=jnp.float32), left_side=True, lower=True)
    global_rows = row_index * root_rows + jnp.arange(root_rows, dtype=jnp.int32)
    global_cols = group_index * root_cols + jnp.arange(root_cols, dtype=jnp.int32)
    left = lax.dot_general(row_raw, inverse, (((1,), (1,)), ((), ())), precision=high)
    right = lax.dot_general(inverse, col_raw, (((1,), (0,)), ((), ())), precision=high)
    update = lax.dot_general(left, right, (((1,), (0,)), ((), ())), precision=high)
    trailing_mask = (global_rows[:, None] >= RP) & (global_cols[None, :] >= RP)
    trailing = assembled - jnp.where(trailing_mask, update, 0.0)
    leading = jnp.pad(factor, ((0, root_rows - RP), (0, 0)))
    panel = jnp.where(global_rows[:, None] < RP, leading, left)
    panel_cols = jnp.where(group_index == 0, panel, trailing[:, :RP])
    return jnp.concatenate([panel_cols, trailing[:, RP:]], axis=1)


def solution(mesh):
    return jax.shard_map(
        shards,
        mesh=mesh,
        in_specs=(
            P("half", "prow", "pcol"),
            P("half", "prow", None),
            P("prow", ("half", "pcol")),
            P(),
        ),
        out_specs=P("prow", ("half", "pcol")),
        check_vma=False,
    )
```

```python
import functools

import jax
import jax.numpy as jnp
from jax import lax
from jax.experimental import pallas as pl
from jax.experimental.pallas import tpu as pltpu
from jax.sharding import PartitionSpec as P

BLK = 128
RP = 256
HALF = BLK // 2
NZ = 8
CHUNKS = 32
TILE = 256
MESH = pl.DeviceIdType.MESH
ANY = pl.BlockSpec(memory_space=pl.ANY)


def position():
    return lax.axis_index("half"), lax.axis_index("prow"), lax.axis_index("pcol")


def greet(devices):
    barrier = pltpu.get_barrier_semaphore()
    for device in devices:
        pl.semaphore_signal(barrier, inc=1, device_id=device, device_id_type=MESH)
    pl.semaphore_wait(barrier, len(devices))


def split(value):
    high = value.astype(jnp.bfloat16)
    return high, (value - high.astype(jnp.float32)).astype(jnp.bfloat16)


def dot3(left, right, dims):
    dot = functools.partial(
        lax.dot_general, dimension_numbers=(dims, ((), ())), preferred_element_type=jnp.float32)
    return dot(left[0], right[0]) + (dot(left[0], right[1]) + dot(left[1], right[0]))


def spread_kernel(leaves, panel, update, outgoing, cols, through, high, low, both, away,
                  ring_send, ring_recv, hand_send, hand_recv, side_send, swap_send, swap_recv):
    core, prow, pcol = position()
    z, x = prow // 2, prow % 2
    partner = (1 - core, prow, pcol)
    upper = (core, ((z + 1) % NZ) * 2 + x, pcol)
    lower = (core, ((z + NZ - 1) % NZ) * 2 + x, pcol)
    beside = z * 2 + (1 - x)
    across = (pcol + 4) % 8
    greet((upper, lower, partner, (0, beside, across), (1, beside, across)))
    ahead = (core, ((z + 1 + (NZ - 2) * core) % NZ) * 2 + x, pcol)
    size = panel.shape[0]
    rows = size // CHUNKS
    above = (z + NZ - pcol) % NZ
    far = jnp.where(core == 0, above, (pcol + NZ - z) % NZ)
    which = jnp.where(core == 0, x, 1 - x)
    at_source = above == 0
    from_side = z == across

    def piece(index):
        return pl.ds(pl.multiple_of(index * rows, rows), rows)

    def own_ring(index, source):
        return pltpu.make_async_remote_copy(
            source, cols.at[which, piece(index)], ring_send.at[0, index],
            ring_recv.at[core, index], device_id=ahead, device_id_type=MESH)

    def pass_ring(index):
        return pltpu.make_async_remote_copy(
            through.at[piece(index)], through.at[piece(index)], ring_send.at[1, index],
            ring_recv.at[1 - core, index], device_id=ahead, device_id_type=MESH)

    def hand(index):
        return pltpu.make_async_remote_copy(
            through.at[piece(index)], cols.at[which, piece(index)], hand_send.at[index],
            hand_recv.at[index], device_id=partner, device_id_type=MESH)

    def feed(index):
        return pltpu.make_async_remote_copy(
            panel.at[piece(index)], through.at[piece(index)], side_send.at[index],
            ring_recv.at[1, index], device_id=(0, prow, pcol), device_id_type=MESH)

    def side_own(index):
        return pltpu.make_async_remote_copy(
            panel.at[piece(index)], cols.at[x, piece(index)], side_send.at[index],
            ring_recv.at[1, index], device_id=(1, beside, across), device_id_type=MESH)

    def side_pass(index):
        return pltpu.make_async_remote_copy(
            panel.at[piece(index)], through.at[piece(index)], side_send.at[index],
            ring_recv.at[0, index], device_id=(1, beside, across), device_id_type=MESH)

    def each(body):
        @pl.loop(0, CHUNKS)
        def _(index):
            body(index)

    @pl.when(from_side & (core == 1))
    def _():
        each(lambda index: side_own(index).start())

    @pl.when(from_side & (core == 0))
    def _():
        each(lambda index: side_pass(index).start())

    @pl.when(at_source & (core == 1))
    def _():
        each(lambda index: feed(index).start())

    head = at_source & (core == 0)
    last = far == NZ - 1

    @pl.loop(0, CHUNKS)
    def _(index):
        here = piece(index)

        @pl.when(head)
        def _():
            own_ring(index, panel.at[here]).start()

        @pl.when(jnp.logical_not(head))
        def _():
            copy = own_ring(index, cols.at[which, here])
            copy.wait_recv()

            @pl.when(jnp.logical_not(last))
            def _():
                copy.start()

        copy = pass_ring(index)
        copy.wait_recv()

        @pl.when(jnp.logical_not(last))
        def _():
            copy.start()

        @pl.when(jnp.logical_not(head))
        def _():
            hand(index).start()

    @pl.when(at_source)
    def _():
        cols[x] = panel[...]

    high[...], low[...] = split(panel[...])

    def multiply(tile):
        columns = cols[tile * TILE // size, pl.ds(tile * TILE % size, TILE)]
        product = dot3((high[...], low[...]), split(columns), ((1,), (1,)))
        place = pl.ds(tile * TILE, TILE)
        value = update[:, place] - product
        for block in range(size // BLK):
            top = value[block * BLK : block * BLK + HALF]
            bottom = value[block * BLK + HALF : (block + 1) * BLK]
            both[core, block, :, place] = jnp.where(core == 0, top, bottom)
            away[block, :, place] = jnp.where(core == 0, bottom, top)

    @pl.when(jnp.logical_not(at_source & (core == 1)))
    def _():
        def arrive(index):
            pltpu.make_async_remote_copy(
                through.at[piece(index)], cols.at[1 - which, piece(index)], hand_send.at[index],
                hand_recv.at[index], device_id=partner, device_id_type=MESH).wait_recv()

        each(arrive)

    for tile in range(2 * size // TILE):
        multiply(tile)
    swap = pltpu.make_async_remote_copy(
        away, both.at[core], swap_send, swap_recv, device_id=partner, device_id_type=MESH)
    swap.start()

    @pl.when(jnp.logical_not(last))
    def _():
        each(lambda index: own_ring(index, panel.at[piece(index)]).wait_send())
        each(lambda index: pass_ring(index).wait_send())

    @pl.when(jnp.logical_not(head))
    def _():
        each(lambda index: hand(index).wait_send())

    @pl.when(from_side | (at_source & (core == 1)))
    def _():
        each(lambda index: feed(index).wait_send())

    swap.wait_send()
    pltpu.make_async_remote_copy(
        away, both.at[1 - core], swap_send, swap_recv, device_id=partner,
        device_id_type=MESH).wait_recv()
    for target in range(outgoing.shape[0]):
        leaf = leaves[target]
        outgoing[target] = both[leaf // 4, leaf % 4]


def spread(leaves, panel, update):
    rows, depth = panel.shape
    width = update.shape[1]
    blocks = rows // BLK
    sems = pltpu.SemaphoreType.DMA((CHUNKS,))
    vmem = pl.BlockSpec(memory_space=pltpu.VMEM)
    return pl.pallas_call(
        spread_kernel,
        out_shape=jax.ShapeDtypeStruct((leaves.shape[0], HALF, width), jnp.float32),
        in_specs=[pl.BlockSpec(memory_space=pltpu.SMEM), vmem, vmem],
        out_specs=vmem,
        scratch_shapes=[
            pltpu.VMEM((2, rows, depth), jnp.float32),
            pltpu.VMEM((rows, depth), jnp.float32),
            pltpu.VMEM((rows, depth), jnp.bfloat16),
            pltpu.VMEM((rows, depth), jnp.bfloat16),
            pltpu.VMEM((2, blocks, HALF, width), jnp.float32),
            pltpu.VMEM((blocks, HALF, width), jnp.float32),
        ] + [pltpu.SemaphoreType.DMA((2, CHUNKS))] * 2 + [sems] * 3
        + [pltpu.SemaphoreType.DMA] * 2,
        compiler_params=pltpu.CompilerParams(collective_id=0, has_side_effects=True),
    )(leaves, panel, update)


def deal_kernel(rows, cols, arrived, out):
    child = pl.program_id(0)
    for group in range(out.shape[0]):
        start = pl.multiple_of(cols[child, group] * BLK, BLK)
        out[group, 0, 0] = arrived[0, :, pl.ds(start, BLK)]


def deal(rows, cols, arrived, groups, slots):
    width = arrived.shape[2]
    return pl.pallas_call(
        deal_kernel,
        out_shape=jax.ShapeDtypeStruct((groups, 2, slots, HALF, BLK), jnp.float32),
        grid_spec=pltpu.PrefetchScalarGridSpec(
            num_scalar_prefetch=2,
            grid=(2, slots),
            in_specs=[
                pl.BlockSpec((1, HALF, width), lambda c, i, rows, cols: (rows[c, i], 0, 0))],
            out_specs=pl.BlockSpec(
                (groups, 1, 1, HALF, BLK), lambda c, i, rows, cols: (0, c, i, 0, 0)),
        ),
    )(rows, cols, arrived)


def extend_kernel(source, row_there, col_there, root, *refs):
    parts, (out, row_raw, col_raw) = refs[:4], refs[4:]
    column = pl.program_id(0)
    for slot in range(out.shape[0] // BLK):
        for half in range(2):
            rows = pl.ds(slot * BLK + half * HALF, HALF)
            value = root[rows, :]
            for child in range(2):
                there = row_there[child, slot] * col_there[child, column] > 0
                part = parts[child * 2 + half][0, 0, slot]
                value = value + jnp.where(there, part, 0.0)
            out[rows, :] = value
            if slot < RP // BLK:
                col_raw[rows, :] = value

    @pl.when(column < RP // BLK)
    def _():
        row_raw[...] = out[...]


def extend(source, row_there, col_there, root, incoming):
    rows, cols = root.shape
    slots = cols // BLK
    groups = incoming.shape[0] // 2

    def part(child, half):
        return pl.BlockSpec(
            (1, 1, rows // BLK, HALF, BLK),
            lambda j, source, *_: (half * groups + source[child, j], child, 0, 0, 0))

    column = pl.BlockSpec((rows, BLK), lambda j, *_: (0, j))
    return pl.pallas_call(
        extend_kernel,
        out_shape=(jax.ShapeDtypeStruct(root.shape, jnp.float32),
                   jax.ShapeDtypeStruct((rows, RP), jnp.float32),
                   jax.ShapeDtypeStruct((RP, cols), jnp.float32)),
        grid_spec=pltpu.PrefetchScalarGridSpec(
            num_scalar_prefetch=3,
            grid=(slots,),
            in_specs=[column] + [part(c, h) for c in range(2) for h in range(2)],
            out_specs=(column,
                       pl.BlockSpec((rows, BLK), lambda j, *_: (0, jnp.minimum(j, RP // BLK - 1))),
                       pl.BlockSpec((RP, BLK), lambda j, *_: (0, j))),
        ),
    )(source, row_there, col_there, root, *[incoming] * 4)


def remote(source, target, send, recv, device):
    return pltpu.make_async_remote_copy(
        source, target, send, recv, device_id=device, device_id_type=MESH)


def others(me, count, body):
    @pl.loop(1, count)
    def _(step):
        body((me + step) % count)


def neighbours():
    half, prow, pcol = position()

    def in_row(k):
        return (k // 8, prow, k % 8)

    def in_col(k):
        return (half, k, pcol)

    return half * 8 + pcol, prow, in_row, in_col


def pivot_kernel(share, out, first, mid, second, first_send, first_recv, second_send,
                 second_recv, third_send, third_recv):
    count = 16
    group, prow, in_row, in_col = neighbours()
    greet([in_row((group + k) % count) for k in range(1, count)]
          + [in_col((prow + k) % count) for k in range(1, count)])

    def scatter(k):
        return remote(share.at[k], first.at[group], first_send.at[k], first_recv.at[group],
                      in_row(k))

    def across(k):
        return remote(mid, second.at[prow], second_send.at[k], second_recv.at[prow], in_col(k))

    def gather(k):
        return remote(out.at[group], out.at[group], third_send.at[k], third_recv.at[group],
                      in_row(k))

    def arrive(target, recv, k):
        remote(target.at[k], target.at[k], recv.at[k], recv.at[k], in_row((group + 1) % count)).wait_recv()

    others(group, count, lambda k: scatter(k).start())
    first[group] = share[group]
    others(group, count, lambda k: arrive(first, first_recv, k))
    total = first[0]
    for k in range(1, count):
        total = total + first[k]
    mid[...] = total
    second[prow] = total
    others(prow, count, lambda k: across(k).start())
    others(prow, count, lambda k: arrive(second, second_recv, k))
    total = second[0]
    for k in range(1, count):
        total = total + second[k]
    out[group] = total
    others(group, count, lambda k: gather(k).start())
    others(group, count, lambda k: arrive(out, third_recv, k))
    others(group, count, lambda k: scatter(k).wait_send())
    others(prow, count, lambda k: across(k).wait_send())
    others(group, count, lambda k: gather(k).wait_send())


def pivot_sum(share):
    count = 16
    rows = RP // count
    many = pltpu.SemaphoreType.DMA((count,))
    vmem = pl.BlockSpec(memory_space=pltpu.VMEM)
    pieces = pltpu.VMEM((count, rows, RP), jnp.float32)
    return pl.pallas_call(
        pivot_kernel,
        out_shape=jax.ShapeDtypeStruct((count, rows, RP), jnp.float32),
        in_specs=[vmem],
        out_specs=vmem,
        scratch_shapes=[pieces, pltpu.VMEM((rows, RP), jnp.float32), pieces] + [many] * 6,
        compiler_params=pltpu.CompilerParams(collective_id=2, has_side_effects=True),
    )(share.reshape(count, rows, RP)).reshape(RP, RP)


def share_kernel(row_raw, col_raw, row_out, col_out, row_cast, row_in, row_send, row_recv,
                 col_cast, col_in, col_send, col_recv):
    count = 16
    group, prow, in_row, in_col = neighbours()
    greet([in_row((group + k) % count) for k in range(1, count)]
          + [in_col((prow + k) % count) for k in range(1, count)])

    def row_first(k):
        return remote(row_raw.at[k], row_out.at[k], row_cast.at[k], row_in, in_row(k))

    def row_second(k):
        return remote(row_out.at[group], row_out.at[group], row_send.at[k], row_recv.at[group],
                      in_row(k))

    def col_first(k):
        return remote(col_raw.at[k], col_out.at[k], col_cast.at[k], col_in, in_col(k))

    def col_second(k):
        return remote(col_out.at[prow], col_out.at[prow], col_send.at[k], col_recv.at[prow],
                      in_col(k))

    def row_start(k):
        return remote(row_raw.at[0], row_out.at[0], row_send.at[k], row_recv.at[0], in_row(k))

    def col_start(k):
        return remote(col_raw.at[0], col_out.at[0], col_send.at[k], col_recv.at[0], in_col(k))

    def spare_first(k, body):
        @pl.when(k > 0)
        def _():
            body()

    @pl.when(group == 0)
    def _():
        others(group, count, lambda k: row_first(k).start())

    @pl.when(prow == 0)
    def _():
        others(prow, count, lambda k: col_first(k).start())

    @pl.when(group == 0)
    def _():
        others(group, count, lambda k: row_start(k).start())
        row_out[...] = row_raw[...]

    @pl.when(prow == 0)
    def _():
        others(prow, count, lambda k: col_start(k).start())
        col_out[...] = col_raw[...]

    @pl.when(group > 0)
    def _():
        row_first(group).wait_recv()
        others(group, count, lambda k: spare_first(k, lambda: row_second(k).start()))

    @pl.when(prow > 0)
    def _():
        col_first(prow).wait_recv()
        others(prow, count, lambda k: spare_first(k, lambda: col_second(k).start()))

    def arrive(target, recv, k):
        remote(target.at[k], target.at[k], recv.at[k], recv.at[k], in_row((group + 1) % count)).wait_recv()

    @pl.when(group > 0)
    def _():
        others(group, count, lambda k: arrive(row_out, row_recv, k))

    @pl.when(prow > 0)
    def _():
        others(prow, count, lambda k: arrive(col_out, col_recv, k))

    @pl.when(group == 0)
    def _():
        others(group, count, lambda k: row_first(k).wait_send())

    @pl.when(prow == 0)
    def _():
        others(prow, count, lambda k: col_first(k).wait_send())

    others(group, count, lambda k: spare_first(k, lambda: row_second(k).wait_send()))
    others(prow, count, lambda k: spare_first(k, lambda: col_second(k).wait_send()))


def share(row_raw, col_raw):
    count = 16
    one, many = pltpu.SemaphoreType.DMA, pltpu.SemaphoreType.DMA((count,))
    vmem = pl.BlockSpec(memory_space=pltpu.VMEM)
    rows, cols = row_raw.shape[0], col_raw.shape[1]
    row_shape = (count, rows // count, RP)
    col_shape = (count, RP // count, cols)
    row_out, col_out = pl.pallas_call(
        share_kernel,
        out_shape=(jax.ShapeDtypeStruct(row_shape, jnp.float32),
                   jax.ShapeDtypeStruct(col_shape, jnp.float32)),
        in_specs=[vmem, vmem],
        out_specs=(vmem, vmem),
        scratch_shapes=[many, one, many, many, many, one, many, many],
        compiler_params=pltpu.CompilerParams(collective_id=1, has_side_effects=True),
    )(row_raw.reshape(row_shape), col_raw.reshape(col_shape))
    return row_out.reshape(rows, RP), col_out.reshape(RP, cols)


def find(labels, wanted, values):
    hit = labels[..., None, :] == wanted[:, None]
    return jnp.sum(jnp.where(hit, values, 0), axis=-1).astype(jnp.int32), jnp.any(hit, axis=-1)


def shards(child_update, child_panel, root_front, index_map):
    rows_dev, cols_dev = child_update.shape[1:]
    root_rows, root_cols = root_front.shape
    row_count, col_count, groups = 16, 8, 16
    row_index = lax.axis_index("prow")
    col_index = lax.axis_index("pcol")
    group_index = lax.axis_index(("half", "pcol"))
    row_slots, col_slots = root_rows // BLK, root_cols // BLK
    child_blocks, col_blocks = rows_dev // BLK, cols_dev // BLK
    blocks = jnp.arange(index_map.shape[1], dtype=jnp.int32)
    everyone = jnp.arange(row_count, dtype=jnp.int32)

    own_rows = lax.dynamic_slice_in_dim(index_map, row_index * child_blocks, child_blocks, 1)
    leaves, _ = find(own_rows.reshape(-1) // row_slots, everyone,
                     jnp.arange(2 * child_blocks, dtype=jnp.int32))
    row_source, row_there = find(
        index_map, row_index * row_slots + jnp.arange(row_slots, dtype=jnp.int32),
        blocks // child_blocks)
    own_cols = lax.dynamic_slice_in_dim(index_map, col_index * col_blocks, col_blocks, 1)
    col_leaves, _ = find(own_cols // col_slots, everyone, jnp.arange(col_blocks, dtype=jnp.int32))
    col_source, col_there = find(
        index_map, group_index * col_slots + jnp.arange(col_slots, dtype=jnp.int32),
        blocks // col_blocks)

    outgoing = spread(leaves, child_panel[0], child_update[0])
    arrived = lax.all_to_all(outgoing, "prow", split_axis=0, concat_axis=0, tiled=True)

    lead = own_rows.reshape(-1)
    lead_hit = lead < RP // BLK
    lead_row = jnp.sum(jnp.where(lead_hit, lead, 0))
    lead_child = jnp.sum(jnp.where(lead_hit, jnp.arange(lead.shape[0]) // child_blocks, 0))
    lead_cols = lax.dynamic_index_in_dim(own_cols, lead_child, 0, keepdims=False)
    col_hit = lead_cols < RP // BLK
    lead_col = jnp.sum(jnp.where(col_hit, lead_cols, 0))
    lead_start = jnp.sum(jnp.where(col_hit, jnp.arange(col_blocks) * BLK, 0))
    lead_block = lax.dynamic_slice(outgoing, (0, 0, lead_start), (1, HALF, BLK))[0]
    lead_block = jnp.where(jnp.any(lead_hit) & jnp.any(col_hit), lead_block, 0.0)
    lead_root = jnp.where((row_index == 0) & (group_index == 0), root_front[:RP, :RP], 0.0)
    at = (lead_row * BLK + lax.axis_index("half") * HALF, lead_col * BLK)
    lead_part = lax.dynamic_update_slice(
        lead_root, lead_block + lax.dynamic_slice(lead_root, at, (HALF, BLK)), at)
    pivot, arrived = lax.optimization_barrier((pivot_sum(lead_part), arrived))
    factor = jnp.linalg.cholesky(pivot)
    inverse = lax.linalg.triangular_solve(
        factor, jnp.eye(RP, dtype=jnp.float32), left_side=True, lower=True)

    dealt = deal(row_source, col_leaves, arrived, groups, row_slots)
    incoming = lax.all_to_all(dealt, ("half", "pcol"), split_axis=0, concat_axis=0, tiled=True)
    assembled, row_raw, col_raw = extend(
        col_source, row_there.astype(jnp.int32), col_there.astype(jnp.int32), root_front, incoming)
    row_raw, col_raw = share(row_raw, col_raw)

    high = lax.Precision.HIGH
    global_rows = row_index * root_rows + jnp.arange(root_rows, dtype=jnp.int32)
    global_cols = group_index * root_cols + jnp.arange(root_cols, dtype=jnp.int32)
    left = lax.dot_general(row_raw, inverse, (((1,), (1,)), ((), ())), precision=high)
    right = lax.dot_general(inverse, col_raw, (((1,), (0,)), ((), ())), precision=high)
    update = lax.dot_general(left, right, (((1,), (0,)), ((), ())), precision=high)
    trailing_mask = (global_rows[:, None] >= RP) & (global_cols[None, :] >= RP)
    trailing = assembled - jnp.where(trailing_mask, update, 0.0)
    leading = jnp.pad(factor, ((0, root_rows - RP), (0, 0)))
    panel = jnp.where(global_rows[:, None] < RP, leading, left)
    panel_cols = jnp.where(group_index == 0, panel, trailing[:, :RP])
    return jnp.concatenate([panel_cols, trailing[:, RP:]], axis=1)


def solution(mesh):
    return jax.shard_map(
        shards,
        mesh=mesh,
        in_specs=(
            P("half", "prow", "pcol"),
            P("half", "prow", None),
            P("prow", ("half", "pcol")),
            P(),
        ),
        out_specs=P("prow", ("half", "pcol")),
        check_vma=False,
    )
```

```python
import functools

import jax
import jax.numpy as jnp
from jax import lax
from jax.experimental import pallas as pl
from jax.experimental.pallas import tpu as pltpu
from jax.sharding import PartitionSpec as P

BLK = 128
RP = 256
HALF = BLK // 2
NZ = 8
CHUNKS = 32
TILE = 256
COUNT = 16
SLOTS = 6
PARTS = 4
PART = HALF // PARTS
MESH = pl.DeviceIdType.MESH
ANY = pl.BlockSpec(memory_space=pl.ANY)


def position():
    return lax.axis_index("half"), lax.axis_index("prow"), lax.axis_index("pcol")


def greet(devices):
    barrier = pltpu.get_barrier_semaphore()
    for device in devices:
        pl.semaphore_signal(barrier, inc=1, device_id=device, device_id_type=MESH)
    pl.semaphore_wait(barrier, len(devices))


def split(value):
    high = value.astype(jnp.bfloat16)
    return high, (value - high.astype(jnp.float32)).astype(jnp.bfloat16)


def dot3(left, right, dims):
    dot = functools.partial(
        lax.dot_general, dimension_numbers=(dims, ((), ())), preferred_element_type=jnp.float32)
    return dot(left[0], right[0]) + (dot(left[0], right[1]) + dot(left[1], right[0]))


def remote(source, target, send, recv, device):
    return pltpu.make_async_remote_copy(
        source, target, send, recv, device_id=device, device_id_type=MESH)


def others(me, count, body):
    @pl.loop(1, count)
    def _(step):
        body((me + step) % count)


def neighbours():
    half, prow, pcol = position()

    def in_row(k):
        return (k // 8, prow, k % 8)

    def in_col(k):
        return (half, k, pcol)

    return half * 8 + pcol, prow, in_row, in_col


def fill(table, value):
    for i in range(table.shape[0]):
        for j in range(table.shape[1]):
            table[i, j] = value


def tables_kernel(index_map, leaves, rows, cols, lead_at, source, row_there, col_there, weight):
    group, prow, _, _ = neighbours()
    pcol = lax.axis_index("pcol")
    total = index_map.shape[1]
    row_blocks, col_blocks = total // COUNT, total // 8
    for table in (leaves, rows, cols, source, row_there, col_there):
        fill(table, 0)

    @pl.loop(0, total)
    def _(b):
        for child in range(2):
            label = index_map[child, b]
            owner = lax.div(label, SLOTS)
            slot = label - owner * SLOTS

            @pl.when(owner == prow)
            def _():
                rows[child, slot] = lax.div(b, row_blocks)
                row_there[child, slot] = 1

            @pl.when(owner == group)
            def _():
                source[child, slot] = lax.div(b, col_blocks)
                col_there[child, slot] = 1

    lead, lead_child = jnp.int32(-1), jnp.int32(0)
    for child in range(2):
        for b in range(row_blocks):
            label = index_map[child, prow * row_blocks + b]
            leaves[0, lax.div(label, SLOTS)] = child * row_blocks + b
            lead_child = jnp.where(label < RP // BLK, child, lead_child)
            lead = jnp.where(label < RP // BLK, label, lead)
        for b in range(col_blocks):
            cols[child, lax.div(index_map[child, pcol * col_blocks + b], SLOTS)] = b
    cross, at = jnp.int32(-1), jnp.int32(0)
    for b in range(col_blocks):
        label = index_map[lead_child, pcol * col_blocks + b]
        at = jnp.where(label < RP // BLK, b, at)
        cross = jnp.where(label < RP // BLK, label, cross)
    lead_at[0, 0] = at
    for i in range(RP // BLK):
        for j in range(RP // BLK):
            hit = jnp.where((lead == i) & (cross == j), 1.0, 0.0)
            weight[i * (RP // BLK) + j] = jnp.full(weight.shape[1:], hit, jnp.float32)


def tables(index_map):
    smem = pl.BlockSpec(memory_space=pltpu.SMEM)
    vmem = pl.BlockSpec(memory_space=pltpu.VMEM)
    shapes = [(1, COUNT), (2, SLOTS), (2, COUNT), (1, 1)] + [(2, SLOTS)] * 3
    return pl.pallas_call(
        tables_kernel,
        out_shape=[jax.ShapeDtypeStruct(shape, jnp.int32) for shape in shapes]
        + [jax.ShapeDtypeStruct(((RP // BLK) ** 2, 8, BLK), jnp.float32)],
        in_specs=[smem],
        out_specs=[smem] * len(shapes) + [vmem],
    )(index_map)


def spread_kernel(leaves, panel, update, outgoing, cols, through, high, low, both, away,
                  ring_send, ring_recv, hand_send, hand_recv, side_send, swap_send, swap_recv):
    core, prow, pcol = position()
    z, x = prow // 2, prow % 2
    partner = (1 - core, prow, pcol)
    upper = (core, ((z + 1) % NZ) * 2 + x, pcol)
    lower = (core, ((z + NZ - 1) % NZ) * 2 + x, pcol)
    beside = z * 2 + (1 - x)
    across = (pcol + 4) % 8
    greet((upper, lower, partner, (0, beside, across), (1, beside, across)))
    ahead = (core, ((z + 1 + (NZ - 2) * core) % NZ) * 2 + x, pcol)
    size = panel.shape[0]
    rows = size // CHUNKS
    above = (z + NZ - pcol) % NZ
    far = jnp.where(core == 0, above, (pcol + NZ - z) % NZ)
    which = jnp.where(core == 0, x, 1 - x)
    at_source = above == 0
    from_side = z == across

    def piece(index):
        return pl.ds(pl.multiple_of(index * rows, rows), rows)

    def own_ring(index, source):
        return pltpu.make_async_remote_copy(
            source, cols.at[which, piece(index)], ring_send.at[0, index],
            ring_recv.at[core, index], device_id=ahead, device_id_type=MESH)

    def pass_ring(index):
        return pltpu.make_async_remote_copy(
            through.at[piece(index)], through.at[piece(index)], ring_send.at[1, index],
            ring_recv.at[1 - core, index], device_id=ahead, device_id_type=MESH)

    def hand(index):
        return pltpu.make_async_remote_copy(
            through.at[piece(index)], cols.at[which, piece(index)], hand_send.at[index],
            hand_recv.at[index], device_id=partner, device_id_type=MESH)

    def feed(index):
        return pltpu.make_async_remote_copy(
            panel.at[piece(index)], through.at[piece(index)], side_send.at[index],
            ring_recv.at[1, index], device_id=(0, prow, pcol), device_id_type=MESH)

    def side_own(index):
        return pltpu.make_async_remote_copy(
            panel.at[piece(index)], cols.at[x, piece(index)], side_send.at[index],
            ring_recv.at[1, index], device_id=(1, beside, across), device_id_type=MESH)

    def side_pass(index):
        return pltpu.make_async_remote_copy(
            panel.at[piece(index)], through.at[piece(index)], side_send.at[index],
            ring_recv.at[0, index], device_id=(1, beside, across), device_id_type=MESH)

    def each(body):
        @pl.loop(0, CHUNKS)
        def _(index):
            body(index)

    @pl.when(from_side & (core == 1))
    def _():
        each(lambda index: side_own(index).start())

    @pl.when(from_side & (core == 0))
    def _():
        each(lambda index: side_pass(index).start())

    @pl.when(at_source & (core == 1))
    def _():
        each(lambda index: feed(index).start())

    head = at_source & (core == 0)
    last = far == NZ - 1

    @pl.loop(0, CHUNKS)
    def _(index):
        here = piece(index)

        @pl.when(head)
        def _():
            own_ring(index, panel.at[here]).start()

        @pl.when(jnp.logical_not(head))
        def _():
            copy = own_ring(index, cols.at[which, here])
            copy.wait_recv()

            @pl.when(jnp.logical_not(last))
            def _():
                copy.start()

        copy = pass_ring(index)
        copy.wait_recv()

        @pl.when(jnp.logical_not(last))
        def _():
            copy.start()

        @pl.when(jnp.logical_not(head))
        def _():
            hand(index).start()

    @pl.when(at_source)
    def _():
        cols[x] = panel[...]

    high[...], low[...] = split(panel[...])

    def multiply(tile):
        columns = cols[tile * TILE // size, pl.ds(tile * TILE % size, TILE)]
        product = dot3((high[...], low[...]), split(columns), ((1,), (1,)))
        place = pl.ds(tile * TILE, TILE)
        value = update[:, place] - product
        for block in range(size // BLK):
            top = value[block * BLK : block * BLK + HALF]
            bottom = value[block * BLK + HALF : (block + 1) * BLK]
            both[core, block, :, place] = jnp.where(core == 0, top, bottom)
            away[block, :, place] = jnp.where(core == 0, bottom, top)

    @pl.when(jnp.logical_not(at_source & (core == 1)))
    def _():
        def arrive(index):
            pltpu.make_async_remote_copy(
                through.at[piece(index)], cols.at[1 - which, piece(index)], hand_send.at[index],
                hand_recv.at[index], device_id=partner, device_id_type=MESH).wait_recv()

        each(arrive)

    for tile in range(2 * size // TILE):
        multiply(tile)
    swap = pltpu.make_async_remote_copy(
        away, both.at[core], swap_send, swap_recv, device_id=partner, device_id_type=MESH)
    swap.start()

    @pl.when(jnp.logical_not(last))
    def _():
        each(lambda index: own_ring(index, panel.at[piece(index)]).wait_send())
        each(lambda index: pass_ring(index).wait_send())

    @pl.when(jnp.logical_not(head))
    def _():
        each(lambda index: hand(index).wait_send())

    @pl.when(from_side | (at_source & (core == 1)))
    def _():
        each(lambda index: feed(index).wait_send())

    swap.wait_send()
    pltpu.make_async_remote_copy(
        away, both.at[1 - core], swap_send, swap_recv, device_id=partner,
        device_id_type=MESH).wait_recv()
    blocks = size // BLK
    for target in range(outgoing.shape[1]):
        leaf = leaves[0, target]
        value = both[leaf // blocks, leaf % blocks]
        for part in range(PARTS):
            for block in range(outgoing.shape[2]):
                outgoing[part, target, block] = value[
                    part * PART : (part + 1) * PART, block * BLK : (block + 1) * BLK]


def spread(leaves, panel, update):
    rows, depth = panel.shape
    width = update.shape[1]
    blocks = rows // BLK
    sems = pltpu.SemaphoreType.DMA((CHUNKS,))
    vmem = pl.BlockSpec(memory_space=pltpu.VMEM)
    return pl.pallas_call(
        spread_kernel,
        out_shape=jax.ShapeDtypeStruct(
            (PARTS, COUNT, width // BLK, PART, BLK), jnp.float32),
        in_specs=[pl.BlockSpec(memory_space=pltpu.SMEM), vmem, vmem],
        out_specs=vmem,
        scratch_shapes=[
            pltpu.VMEM((2, rows, depth), jnp.float32),
            pltpu.VMEM((rows, depth), jnp.float32),
            pltpu.VMEM((rows, depth), jnp.bfloat16),
            pltpu.VMEM((rows, depth), jnp.bfloat16),
            pltpu.VMEM((2, blocks, HALF, width), jnp.float32),
            pltpu.VMEM((blocks, HALF, width), jnp.float32),
        ] + [pltpu.SemaphoreType.DMA((2, CHUNKS))] * 2 + [sems] * 3
        + [pltpu.SemaphoreType.DMA] * 2,
        compiler_params=pltpu.CompilerParams(collective_id=0, has_side_effects=True),
    )(leaves, panel, update)


def eliminate(a, w):
    size = a.shape[0]
    lane = lax.broadcasted_iota(jnp.int32, (size, size), 1)
    line = lax.broadcasted_iota(jnp.int32, (size, size), 0)
    head = lax.broadcasted_iota(jnp.int32, (1, size), 1)
    side = lax.broadcasted_iota(jnp.int32, (size, 1), 0)
    w[...] = jnp.where(lane == line, 1.0, 0.0)

    @pl.loop(0, size)
    def _(j):
        value = a[...]
        column = jnp.sum(jnp.where(lane == j, value, 0.0), axis=1, keepdims=True)
        row = a[pl.ds(j, 1), :]
        pivot = jnp.sum(jnp.where(head == j, row, 0.0), axis=1, keepdims=True)
        scale = 1.0 / pivot
        column = jnp.where(side > j, column, 0.0)
        a[...] = value - column * (row * scale)
        w[...] = w[...] - column * (w[pl.ds(j, 1), :] * scale)

    value = a[...]
    diagonal = jnp.sum(jnp.where(lane == line, value, 0.0), axis=1, keepdims=True)
    scale = 1.0 / jnp.sqrt(diagonal)
    return jnp.where(lane >= line, value * scale, 0.0), w[...] * scale


def dot_full(left, right, dims):
    return lax.dot_general(left, right, (dims, ((), ())), precision=lax.Precision.HIGHEST,
                           preferred_element_type=jnp.float32)


def exchange_kernel(rows, cols, lead_at, weight, outgoing, root_pivot, incoming, factor,
                    inverse, dealt, share, first, mid, second, pivot, a, w, row_send, row_recv,
                    col_send, col_recv, first_send, first_recv, second_send, second_recv,
                    third_send, third_recv, *arrived):
    count = COUNT
    core = lax.axis_index("half")
    group, prow, in_row, in_col = neighbours()

    def row_copy(part, k):
        return remote(outgoing.at[part, k], arrived[part].at[prow],
                      row_send.at[part, k], row_recv.at[part, prow], in_col(k))

    def col_copy(part, k):
        return remote(dealt.at[part, k], incoming.at[part, group], col_send.at[part, k],
                      col_recv.at[part, group], in_row(k))

    def scatter(k):
        return remote(share.at[k], first.at[group], first_send.at[k], first_recv.at[group],
                      in_row(k))

    def across(k):
        return remote(mid, second.at[prow], second_send.at[k], second_recv.at[prow], in_col(k))

    def gather(k):
        return remote(pivot.at[group], pivot.at[group], third_send.at[k], third_recv.at[group],
                      in_row(k))

    def row_wait(target, recv, k):
        remote(target, target, recv, recv, in_row((group + 1) % count)).wait_recv()

    def col_wait(target, recv, k):
        remote(target, target, recv, recv, in_col((prow + 1) % count)).wait_recv()

    def send_rows(part):
        others(prow, count, lambda k: row_copy(part, k).start())
        arrived[part][prow] = outgoing[part, prow]

    def deal(part):
        others(prow, count, lambda k: col_wait(arrived[part].at[k], row_recv.at[part, k], k))

        @pl.loop(0, 2 * SLOTS)
        def _(item):
            child, slot = item // SLOTS, item % SLOTS
            row = rows[child, slot]
            for target in range(count):
                dealt[part, target, child, slot] = arrived[part][row, cols[child, target]]

        others(group, count, lambda k: col_copy(part, k).start())
        incoming[part, group] = dealt[part, group]

    greet([in_row((group + k) % count) for k in range(1, count)]
          + [in_col((prow + k) % count) for k in range(1, count)])
    send_rows(0)

    share[...] = jnp.where((group == 0) & (prow == 0), root_pivot[...], 0.0)
    for part in range(PARTS):
        block = outgoing[part, 0, lead_at[0, 0]]
        for i in range(RP // BLK):
            line = i * (BLK // PART) + core * PARTS + part
            for j in range(RP // BLK):
                here = pl.ds(j * BLK, BLK)
                scale = weight[i * (RP // BLK) + j, 0:1, :]
                share[line, :, here] = share[line, :, here] + block * scale
    others(group, count, lambda k: scatter(k).start())
    first[group] = share[group]
    others(group, count, lambda k: row_wait(first.at[k], first_recv.at[k], k))
    value = first[0]
    for k in range(1, count):
        value = value + first[k]
    mid[...] = value
    second[prow] = value
    others(prow, count, lambda k: across(k).start())
    for part in range(1, PARTS):
        send_rows(part)

    others(prow, count, lambda k: col_wait(second.at[k], second_recv.at[k], k))
    value = second[0]
    for k in range(1, count):
        value = value + second[k]
    pivot[group] = value
    others(group, count, lambda k: gather(k).start())
    deal(0)
    others(group, count, lambda k: row_wait(pivot.at[k], third_recv.at[k], k))
    top, bottom = slice(0, BLK), slice(BLK, RP)
    whole = pivot[...].reshape(RP, RP)
    a[...] = whole[top, top]
    upper, upper_inverse = eliminate(a, w)
    low = dot_full(whole[bottom, top], upper_inverse, ((1,), (1,)))
    factor[top, top] = upper.T
    factor[top, bottom] = jnp.zeros((BLK, BLK), jnp.float32)
    factor[bottom, top] = low
    inverse[top, top] = upper_inverse
    inverse[top, bottom] = jnp.zeros((BLK, BLK), jnp.float32)
    a[...] = whole[bottom, bottom] - dot_full(low, low, ((1,), (1,)))
    deal(1)
    lower, lower_inverse = eliminate(a, w)
    factor[bottom, bottom] = lower.T
    inverse[bottom, bottom] = lower_inverse
    inverse[bottom, top] = -dot_full(
        lower_inverse, dot_full(factor[bottom, top], inverse[top, top], ((1,), (0,))),
        ((1,), (0,)))
    for part in range(2, PARTS):
        deal(part)
    for part in range(PARTS):
        others(group, count, lambda k: row_wait(incoming.at[part, k], col_recv.at[part, k], k))
    for part in range(PARTS):
        others(prow, count, lambda k: row_copy(part, k).wait_send())
        others(group, count, lambda k: col_copy(part, k).wait_send())
    others(group, count, lambda k: scatter(k).wait_send())
    others(prow, count, lambda k: across(k).wait_send())
    others(group, count, lambda k: gather(k).wait_send())


def exchange(rows, cols, lead_at, weight, outgoing, root_pivot):
    count = COUNT
    vmem = pl.BlockSpec(memory_space=pltpu.VMEM)
    smem = pl.BlockSpec(memory_space=pltpu.SMEM)
    shape = (PARTS, count, 2, SLOTS, PART, BLK)
    piece = (RP // count, RP)
    many = pltpu.SemaphoreType.DMA((count,))
    pieces = pltpu.VMEM((count,) + piece, jnp.float32)
    square = jax.ShapeDtypeStruct((RP, RP), jnp.float32)
    return pl.pallas_call(
        exchange_kernel,
        out_shape=(jax.ShapeDtypeStruct(shape, jnp.float32), square, square),
        in_specs=[smem, smem, smem, vmem, vmem, vmem],
        out_specs=(vmem, vmem, vmem),
        scratch_shapes=[pltpu.VMEM(shape, jnp.float32),
                        pieces, pieces, pltpu.VMEM(piece, jnp.float32), pieces, pieces,
                        pltpu.VMEM((BLK, BLK), jnp.float32), pltpu.VMEM((BLK, BLK), jnp.float32)]
        + [pltpu.SemaphoreType.DMA((PARTS, count))] * 4 + [many] * 6
        + [pltpu.VMEM(outgoing.shape[1:], jnp.float32)] * PARTS,
        compiler_params=pltpu.CompilerParams(collective_id=3, has_side_effects=True),
    )(rows, cols, lead_at, weight, outgoing, root_pivot.reshape((count,) + piece))


def extend_kernel(source, row_there, col_there, root, *refs):
    arrivals, (out, row_raw, col_raw) = refs[:4], refs[4:]
    column = pl.program_id(0)
    for slot in range(out.shape[0] // BLK):
        for half in range(2):
            for part in range(PARTS):
                rows = pl.ds(slot * BLK + half * HALF + part * PART, PART)
                value = root[rows, :]
                for child in range(2):
                    there = row_there[child, slot] * col_there[child, column] > 0
                    block = arrivals[child * 2 + half][part, 0, 0, slot]
                    value = value + jnp.where(there, block, 0.0)
                out[rows, :] = value
                if slot < RP // BLK:
                    col_raw[rows, :] = value

    @pl.when(column < RP // BLK)
    def _():
        row_raw[...] = out[...]


def extend(source, row_there, col_there, root, incoming):
    rows, cols = root.shape
    slots = cols // BLK
    groups = incoming.shape[1] // 2

    def part(child, half):
        return pl.BlockSpec(
            (PARTS, 1, 1, rows // BLK, PART, BLK),
            lambda j, source, *_: (0, half * groups + source[child, j], child, 0, 0, 0))

    column = pl.BlockSpec((rows, BLK), lambda j, *_: (0, j))
    return pl.pallas_call(
        extend_kernel,
        out_shape=(jax.ShapeDtypeStruct(root.shape, jnp.float32),
                   jax.ShapeDtypeStruct((rows, RP), jnp.float32),
                   jax.ShapeDtypeStruct((RP, cols), jnp.float32)),
        grid_spec=pltpu.PrefetchScalarGridSpec(
            num_scalar_prefetch=3,
            grid=(slots,),
            in_specs=[column] + [part(c, h) for c in range(2) for h in range(2)],
            out_specs=(column,
                       pl.BlockSpec((rows, BLK), lambda j, *_: (0, jnp.minimum(j, RP // BLK - 1))),
                       pl.BlockSpec((RP, BLK), lambda j, *_: (0, j))),
        ),
    )(source, row_there, col_there, root, *[incoming] * 4)


def share_kernel(row_raw, col_raw, row_out, col_out, row_cast, row_in, row_send, row_recv,
                 col_cast, col_in, col_send, col_recv):
    count = 16
    group, prow, in_row, in_col = neighbours()
    greet([in_row((group + k) % count) for k in range(1, count)]
          + [in_col((prow + k) % count) for k in range(1, count)])

    def row_first(k):
        return remote(row_raw.at[k], row_out.at[k], row_cast.at[k], row_in, in_row(k))

    def row_second(k):
        return remote(row_out.at[group], row_out.at[group], row_send.at[k], row_recv.at[group],
                      in_row(k))

    def col_first(k):
        return remote(col_raw.at[k], col_out.at[k], col_cast.at[k], col_in, in_col(k))

    def col_second(k):
        return remote(col_out.at[prow], col_out.at[prow], col_send.at[k], col_recv.at[prow],
                      in_col(k))

    def row_start(k):
        return remote(row_raw.at[0], row_out.at[0], row_send.at[k], row_recv.at[0], in_row(k))

    def col_start(k):
        return remote(col_raw.at[0], col_out.at[0], col_send.at[k], col_recv.at[0], in_col(k))

    def spare_first(k, body):
        @pl.when(k > 0)
        def _():
            body()

    @pl.when(group == 0)
    def _():
        others(group, count, lambda k: row_first(k).start())

    @pl.when(prow == 0)
    def _():
        others(prow, count, lambda k: col_first(k).start())

    @pl.when(group == 0)
    def _():
        others(group, count, lambda k: row_start(k).start())
        row_out[...] = row_raw[...]

    @pl.when(prow == 0)
    def _():
        others(prow, count, lambda k: col_start(k).start())
        col_out[...] = col_raw[...]

    @pl.when(group > 0)
    def _():
        row_first(group).wait_recv()
        others(group, count, lambda k: spare_first(k, lambda: row_second(k).start()))

    @pl.when(prow > 0)
    def _():
        col_first(prow).wait_recv()
        others(prow, count, lambda k: spare_first(k, lambda: col_second(k).start()))

    def arrive(target, recv, k):
        remote(target.at[k], target.at[k], recv.at[k], recv.at[k], in_row((group + 1) % count)).wait_recv()

    @pl.when(group > 0)
    def _():
        others(group, count, lambda k: arrive(row_out, row_recv, k))

    @pl.when(prow > 0)
    def _():
        others(prow, count, lambda k: arrive(col_out, col_recv, k))

    @pl.when(group == 0)
    def _():
        others(group, count, lambda k: row_first(k).wait_send())

    @pl.when(prow == 0)
    def _():
        others(prow, count, lambda k: col_first(k).wait_send())

    others(group, count, lambda k: spare_first(k, lambda: row_second(k).wait_send()))
    others(prow, count, lambda k: spare_first(k, lambda: col_second(k).wait_send()))


def share(row_raw, col_raw):
    count = 16
    one, many = pltpu.SemaphoreType.DMA, pltpu.SemaphoreType.DMA((count,))
    vmem = pl.BlockSpec(memory_space=pltpu.VMEM)
    rows, cols = row_raw.shape[0], col_raw.shape[1]
    row_shape = (count, rows // count, RP)
    col_shape = (count, RP // count, cols)
    row_out, col_out = pl.pallas_call(
        share_kernel,
        out_shape=(jax.ShapeDtypeStruct(row_shape, jnp.float32),
                   jax.ShapeDtypeStruct(col_shape, jnp.float32)),
        in_specs=[vmem, vmem],
        out_specs=(vmem, vmem),
        scratch_shapes=[many, one, many, many, many, one, many, many],
        compiler_params=pltpu.CompilerParams(collective_id=1, has_side_effects=True),
    )(row_raw.reshape(row_shape), col_raw.reshape(col_shape))
    return row_out.reshape(rows, RP), col_out.reshape(RP, cols)


def shards(child_update, child_panel, root_front, index_map):
    root_rows, root_cols = root_front.shape
    row_index = lax.axis_index("prow")
    group_index = lax.axis_index(("half", "pcol"))
    leaves, rows, cols, lead_at, col_source, row_there, col_there, weight = tables(index_map)
    outgoing = spread(leaves, child_panel[0], child_update[0])
    incoming, factor, inverse = exchange(
        rows, cols, lead_at, weight, outgoing, root_front[:RP, :RP])
    assembled, row_raw, col_raw = extend(col_source, row_there, col_there, root_front, incoming)
    row_raw, col_raw = share(row_raw, col_raw)

    high = lax.Precision.HIGH
    global_rows = row_index * root_rows + jnp.arange(root_rows, dtype=jnp.int32)
    global_cols = group_index * root_cols + jnp.arange(root_cols, dtype=jnp.int32)
    left = lax.dot_general(row_raw, inverse, (((1,), (1,)), ((), ())), precision=high)
    right = lax.dot_general(inverse, col_raw, (((1,), (0,)), ((), ())), precision=high)
    update = lax.dot_general(left, right, (((1,), (0,)), ((), ())), precision=high)
    trailing_mask = (global_rows[:, None] >= RP) & (global_cols[None, :] >= RP)
    trailing = assembled - jnp.where(trailing_mask, update, 0.0)
    leading = jnp.pad(factor, ((0, root_rows - RP), (0, 0)))
    panel = jnp.where(global_rows[:, None] < RP, leading, left)
    panel_cols = jnp.where(group_index == 0, panel, trailing[:, :RP])
    return jnp.concatenate([panel_cols, trailing[:, RP:]], axis=1)


def solution(mesh):
    return jax.shard_map(
        shards,
        mesh=mesh,
        in_specs=(
            P("half", "prow", "pcol"),
            P("half", "prow", None),
            P("prow", ("half", "pcol")),
            P(),
        ),
        out_specs=P("prow", ("half", "pcol")),
        check_vma=False,
    )
```

```python
import functools

import jax
import jax.numpy as jnp
from jax import lax
from jax.experimental import pallas as pl
from jax.experimental.pallas import tpu as pltpu
from jax.sharding import PartitionSpec as P

BLK = 128
RP = 256
HALF = BLK // 2
NZ = 8
CHUNKS = 32
TILE = 256
COUNT = 16
SLOTS = 6
PARTS = 4
PART = HALF // PARTS
MESH = pl.DeviceIdType.MESH
ANY = pl.BlockSpec(memory_space=pl.ANY)


def position():
    return lax.axis_index("half"), lax.axis_index("prow"), lax.axis_index("pcol")


def greet(devices):
    barrier = pltpu.get_barrier_semaphore()
    for device in devices:
        pl.semaphore_signal(barrier, inc=1, device_id=device, device_id_type=MESH)
    pl.semaphore_wait(barrier, len(devices))


def split(value):
    high = value.astype(jnp.bfloat16)
    return high, (value - high.astype(jnp.float32)).astype(jnp.bfloat16)


def dot3(left, right, dims):
    dot = functools.partial(
        lax.dot_general, dimension_numbers=(dims, ((), ())), preferred_element_type=jnp.float32)
    return dot(left[0], right[0]) + (dot(left[0], right[1]) + dot(left[1], right[0]))


def remote(source, target, send, recv, device):
    return pltpu.make_async_remote_copy(
        source, target, send, recv, device_id=device, device_id_type=MESH)


def others(me, count, body):
    @pl.loop(1, count)
    def _(step):
        body((me + step) % count)


def neighbours():
    half, prow, pcol = position()

    def in_row(k):
        return (k // 8, prow, k % 8)

    def in_col(k):
        return (half, k, pcol)

    return half * 8 + pcol, prow, in_row, in_col


def fill(table, value):
    for i in range(table.shape[0]):
        for j in range(table.shape[1]):
            table[i, j] = value


def tables_kernel(index_map, leaves, rows, cols, lead_at, source, weight, there,
                  row_there, col_there):
    group, prow, _, _ = neighbours()
    pcol = lax.axis_index("pcol")
    total = index_map.shape[1]
    row_blocks, col_blocks = total // COUNT, total // 8
    for table in (leaves, rows, cols, source, row_there, col_there):
        fill(table, 0)

    @pl.loop(0, total)
    def _(b):
        for child in range(2):
            label = index_map[child, b]
            owner = lax.div(label, SLOTS)
            slot = label - owner * SLOTS

            @pl.when(owner == prow)
            def _():
                rows[child, slot] = lax.div(b, row_blocks)
                row_there[child, slot] = 1

            @pl.when(owner == group)
            def _():
                source[child, slot] = lax.div(b, col_blocks)
                col_there[child, slot] = 1

    lead, lead_child = jnp.int32(-1), jnp.int32(0)
    for child in range(2):
        for b in range(row_blocks):
            label = index_map[child, prow * row_blocks + b]
            leaves[0, lax.div(label, SLOTS)] = child * row_blocks + b
            lead_child = jnp.where(label < RP // BLK, child, lead_child)
            lead = jnp.where(label < RP // BLK, label, lead)
        for b in range(col_blocks):
            cols[child, lax.div(index_map[child, pcol * col_blocks + b], SLOTS)] = b
    cross, at = jnp.int32(-1), jnp.int32(0)
    for b in range(col_blocks):
        label = index_map[lead_child, pcol * col_blocks + b]
        at = jnp.where(label < RP // BLK, b, at)
        cross = jnp.where(label < RP // BLK, label, cross)
    lead_at[0, 0] = at
    for i in range(RP // BLK):
        for j in range(RP // BLK):
            hit = jnp.where((lead == i) & (cross == j), 1.0, 0.0)
            weight[i * (RP // BLK) + j] = jnp.full(weight.shape[1:], hit, jnp.float32)
    for child in range(2):
        for i in range(SLOTS):
            for j in range(SLOTS):
                hit = jnp.where(row_there[child, i] * col_there[child, j] > 0, 1.0, 0.0)
                there[(child * SLOTS + i) * SLOTS + j] = jnp.full(
                    there.shape[1:], hit, jnp.float32)


def tables(index_map):
    smem = pl.BlockSpec(memory_space=pltpu.SMEM)
    vmem = pl.BlockSpec(memory_space=pltpu.VMEM)
    shapes = [(1, COUNT), (2, SLOTS), (2, COUNT), (1, 1), (2, SLOTS)]
    factors = [((RP // BLK) ** 2, 8, BLK), (2 * SLOTS * SLOTS, 8, BLK)]
    return pl.pallas_call(
        tables_kernel,
        out_shape=[jax.ShapeDtypeStruct(shape, jnp.int32) for shape in shapes]
        + [jax.ShapeDtypeStruct(shape, jnp.float32) for shape in factors],
        in_specs=[smem],
        out_specs=[smem] * len(shapes) + [vmem] * len(factors),
        scratch_shapes=[pltpu.SMEM((2, SLOTS), jnp.int32)] * 2,
    )(index_map)


def spread_kernel(leaves, panel, update, outgoing, cols, through, high, low, both, away,
                  ring_send, ring_recv, hand_send, hand_recv, side_send, swap_send, swap_recv):
    core, prow, pcol = position()
    z, x = prow // 2, prow % 2
    partner = (1 - core, prow, pcol)
    upper = (core, ((z + 1) % NZ) * 2 + x, pcol)
    lower = (core, ((z + NZ - 1) % NZ) * 2 + x, pcol)
    beside = z * 2 + (1 - x)
    across = (pcol + 4) % 8
    greet((upper, lower, partner, (0, beside, across), (1, beside, across)))
    ahead = (core, ((z + 1 + (NZ - 2) * core) % NZ) * 2 + x, pcol)
    size = panel.shape[0]
    rows = size // CHUNKS
    above = (z + NZ - pcol) % NZ
    far = jnp.where(core == 0, above, (pcol + NZ - z) % NZ)
    which = jnp.where(core == 0, x, 1 - x)
    at_source = above == 0
    from_side = z == across

    def piece(index):
        return pl.ds(pl.multiple_of(index * rows, rows), rows)

    def own_ring(index, source):
        return pltpu.make_async_remote_copy(
            source, cols.at[which, piece(index)], ring_send.at[0, index],
            ring_recv.at[core, index], device_id=ahead, device_id_type=MESH)

    def pass_ring(index):
        return pltpu.make_async_remote_copy(
            through.at[piece(index)], through.at[piece(index)], ring_send.at[1, index],
            ring_recv.at[1 - core, index], device_id=ahead, device_id_type=MESH)

    def hand(index):
        return pltpu.make_async_remote_copy(
            through.at[piece(index)], cols.at[which, piece(index)], hand_send.at[index],
            hand_recv.at[index], device_id=partner, device_id_type=MESH)

    def feed(index):
        return pltpu.make_async_remote_copy(
            panel.at[piece(index)], through.at[piece(index)], side_send.at[index],
            ring_recv.at[1, index], device_id=(0, prow, pcol), device_id_type=MESH)

    def side_own(index):
        return pltpu.make_async_remote_copy(
            panel.at[piece(index)], cols.at[x, piece(index)], side_send.at[index],
            ring_recv.at[1, index], device_id=(1, beside, across), device_id_type=MESH)

    def side_pass(index):
        return pltpu.make_async_remote_copy(
            panel.at[piece(index)], through.at[piece(index)], side_send.at[index],
            ring_recv.at[0, index], device_id=(1, beside, across), device_id_type=MESH)

    def each(body):
        @pl.loop(0, CHUNKS)
        def _(index):
            body(index)

    @pl.when(from_side & (core == 1))
    def _():
        each(lambda index: side_own(index).start())

    @pl.when(from_side & (core == 0))
    def _():
        each(lambda index: side_pass(index).start())

    @pl.when(at_source & (core == 1))
    def _():
        each(lambda index: feed(index).start())

    head = at_source & (core == 0)
    last = far == NZ - 1

    @pl.loop(0, CHUNKS)
    def _(index):
        here = piece(index)

        @pl.when(head)
        def _():
            own_ring(index, panel.at[here]).start()

        @pl.when(jnp.logical_not(head))
        def _():
            copy = own_ring(index, cols.at[which, here])
            copy.wait_recv()

            @pl.when(jnp.logical_not(last))
            def _():
                copy.start()

        copy = pass_ring(index)
        copy.wait_recv()

        @pl.when(jnp.logical_not(last))
        def _():
            copy.start()

        @pl.when(jnp.logical_not(head))
        def _():
            hand(index).start()

    @pl.when(at_source)
    def _():
        cols[x] = panel[...]

    high[...], low[...] = split(panel[...])

    def multiply(tile):
        columns = cols[tile * TILE // size, pl.ds(tile * TILE % size, TILE)]
        product = dot3((high[...], low[...]), split(columns), ((1,), (1,)))
        place = pl.ds(tile * TILE, TILE)
        value = update[:, place] - product
        for block in range(size // BLK):
            top = value[block * BLK : block * BLK + HALF]
            bottom = value[block * BLK + HALF : (block + 1) * BLK]
            both[core, block, :, place] = jnp.where(core == 0, top, bottom)
            away[block, :, place] = jnp.where(core == 0, bottom, top)

    @pl.when(jnp.logical_not(at_source & (core == 1)))
    def _():
        def arrive(index):
            pltpu.make_async_remote_copy(
                through.at[piece(index)], cols.at[1 - which, piece(index)], hand_send.at[index],
                hand_recv.at[index], device_id=partner, device_id_type=MESH).wait_recv()

        each(arrive)

    for tile in range(2 * size // TILE):
        multiply(tile)
    swap = pltpu.make_async_remote_copy(
        away, both.at[core], swap_send, swap_recv, device_id=partner, device_id_type=MESH)
    swap.start()

    @pl.when(jnp.logical_not(last))
    def _():
        each(lambda index: own_ring(index, panel.at[piece(index)]).wait_send())
        each(lambda index: pass_ring(index).wait_send())

    @pl.when(jnp.logical_not(head))
    def _():
        each(lambda index: hand(index).wait_send())

    @pl.when(from_side | (at_source & (core == 1)))
    def _():
        each(lambda index: feed(index).wait_send())

    swap.wait_send()
    pltpu.make_async_remote_copy(
        away, both.at[1 - core], swap_send, swap_recv, device_id=partner,
        device_id_type=MESH).wait_recv()
    blocks = size // BLK
    for target in range(outgoing.shape[1]):
        leaf = leaves[0, target]
        value = both[leaf // blocks, leaf % blocks]
        for part in range(PARTS):
            for block in range(outgoing.shape[2]):
                outgoing[part, target, block] = value[
                    part * PART : (part + 1) * PART, block * BLK : (block + 1) * BLK]


def spread(leaves, panel, update):
    rows, depth = panel.shape
    width = update.shape[1]
    blocks = rows // BLK
    sems = pltpu.SemaphoreType.DMA((CHUNKS,))
    vmem = pl.BlockSpec(memory_space=pltpu.VMEM)
    return pl.pallas_call(
        spread_kernel,
        out_shape=jax.ShapeDtypeStruct(
            (PARTS, COUNT, width // BLK, PART, BLK), jnp.float32),
        in_specs=[pl.BlockSpec(memory_space=pltpu.SMEM), vmem, vmem],
        out_specs=vmem,
        scratch_shapes=[
            pltpu.VMEM((2, rows, depth), jnp.float32),
            pltpu.VMEM((rows, depth), jnp.float32),
            pltpu.VMEM((rows, depth), jnp.bfloat16),
            pltpu.VMEM((rows, depth), jnp.bfloat16),
            pltpu.VMEM((2, blocks, HALF, width), jnp.float32),
            pltpu.VMEM((blocks, HALF, width), jnp.float32),
        ] + [pltpu.SemaphoreType.DMA((2, CHUNKS))] * 2 + [sems] * 3
        + [pltpu.SemaphoreType.DMA] * 2,
        compiler_params=pltpu.CompilerParams(collective_id=0, has_side_effects=True),
    )(leaves, panel, update)


def eliminate(a, w):
    size = a.shape[0]
    lane = lax.broadcasted_iota(jnp.int32, (size, size), 1)
    line = lax.broadcasted_iota(jnp.int32, (size, size), 0)
    head = lax.broadcasted_iota(jnp.int32, (1, size), 1)
    side = lax.broadcasted_iota(jnp.int32, (size, 1), 0)
    w[...] = jnp.where(lane == line, 1.0, 0.0)

    @pl.loop(0, size)
    def _(j):
        value = a[...]
        column = jnp.sum(jnp.where(lane == j, value, 0.0), axis=1, keepdims=True)
        row = a[pl.ds(j, 1), :]
        pivot = jnp.sum(jnp.where(head == j, row, 0.0), axis=1, keepdims=True)
        scale = 1.0 / pivot
        column = jnp.where(side > j, column, 0.0)
        a[...] = value - column * (row * scale)
        w[...] = w[...] - column * (w[pl.ds(j, 1), :] * scale)

    value = a[...]
    diagonal = jnp.sum(jnp.where(lane == line, value, 0.0), axis=1, keepdims=True)
    scale = 1.0 / jnp.sqrt(diagonal)
    return jnp.where(lane >= line, value * scale, 0.0), w[...] * scale


def dot_full(left, right, dims):
    return lax.dot_general(left, right, (dims, ((), ())), precision=lax.Precision.HIGHEST,
                           preferred_element_type=jnp.float32)


def exchange_kernel(rows, cols, lead_at, source, weight, there, outgoing, root, out, incoming,
                    factor, inverse, dealt, share, first, mid, second, pivot, a, w, row_panel,
                    col_panel, row_send, row_recv, col_send, col_recv, first_send, first_recv,
                    second_send, second_recv, third_send, third_recv, over_cast, over_in,
                    over_send, over_recv, down_cast, down_in, down_send, down_recv, *arrived):
    count = COUNT
    core = lax.axis_index("half")
    group, prow, in_row, in_col = neighbours()

    def row_copy(part, k):
        return remote(outgoing.at[part, k], arrived[part].at[prow],
                      row_send.at[part, k], row_recv.at[part, prow], in_col(k))

    def col_copy(part, k):
        return remote(dealt.at[part, k], incoming.at[part, group], col_send.at[part, k],
                      col_recv.at[part, group], in_row(k))

    def scatter(k):
        return remote(share.at[k], first.at[group], first_send.at[k], first_recv.at[group],
                      in_row(k))

    def across(k):
        return remote(mid, second.at[prow], second_send.at[k], second_recv.at[prow], in_col(k))

    def gather(k):
        return remote(pivot.at[group], pivot.at[group], third_send.at[k], third_recv.at[group],
                      in_row(k))

    def row_wait(target, recv, k):
        remote(target, target, recv, recv, in_row((group + 1) % count)).wait_recv()

    def col_wait(target, recv, k):
        remote(target, target, recv, recv, in_col((prow + 1) % count)).wait_recv()

    def send_rows(part):
        others(prow, count, lambda k: row_copy(part, k).start())
        arrived[part][prow] = outgoing[part, prow]

    def deal(part):
        others(prow, count, lambda k: col_wait(arrived[part].at[k], row_recv.at[part, k], k))

        @pl.loop(0, 2 * SLOTS)
        def _(item):
            child, slot = item // SLOTS, item % SLOTS
            row = rows[child, slot]
            for target in range(count):
                dealt[part, target, child, slot] = arrived[part][row, cols[child, target]]

        others(group, count, lambda k: col_copy(part, k).start())
        incoming[part, group] = dealt[part, group]

    greet([in_row((group + k) % count) for k in range(1, count)]
          + [in_col((prow + k) % count) for k in range(1, count)])
    send_rows(0)

    share[...] = jnp.where(
        (group == 0) & (prow == 0), root[:RP, :RP].reshape(share.shape), 0.0)
    for part in range(PARTS):
        block = outgoing[part, 0, lead_at[0, 0]]
        for i in range(RP // BLK):
            line = i * (BLK // PART) + core * PARTS + part
            for j in range(RP // BLK):
                here = pl.ds(j * BLK, BLK)
                scale = weight[i * (RP // BLK) + j, 0:1, :]
                share[line, :, here] = share[line, :, here] + block * scale
    others(group, count, lambda k: scatter(k).start())
    first[group] = share[group]
    others(group, count, lambda k: row_wait(first.at[k], first_recv.at[k], k))
    value = first[0]
    for k in range(1, count):
        value = value + first[k]
    mid[...] = value
    second[prow] = value
    others(prow, count, lambda k: across(k).start())
    for part in range(1, PARTS):
        send_rows(part)

    others(prow, count, lambda k: col_wait(second.at[k], second_recv.at[k], k))
    value = second[0]
    for k in range(1, count):
        value = value + second[k]
    pivot[group] = value
    others(group, count, lambda k: gather(k).start())
    deal(0)
    others(group, count, lambda k: row_wait(pivot.at[k], third_recv.at[k], k))
    top, bottom = slice(0, BLK), slice(BLK, RP)
    whole = pivot[...].reshape(RP, RP)
    a[...] = whole[top, top]
    upper, upper_inverse = eliminate(a, w)
    low = dot_full(whole[bottom, top], upper_inverse, ((1,), (1,)))
    factor[top, top] = upper.T
    factor[top, bottom] = jnp.zeros((BLK, BLK), jnp.float32)
    factor[bottom, top] = low
    inverse[top, top] = upper_inverse
    inverse[top, bottom] = jnp.zeros((BLK, BLK), jnp.float32)
    a[...] = whole[bottom, bottom] - dot_full(low, low, ((1,), (1,)))
    deal(1)
    lower, lower_inverse = eliminate(a, w)
    factor[bottom, bottom] = lower.T
    inverse[bottom, bottom] = lower_inverse
    inverse[bottom, top] = -dot_full(
        lower_inverse, dot_full(factor[bottom, top], inverse[top, top], ((1,), (0,))),
        ((1,), (0,)))
    for part in range(2, PARTS):
        deal(part)
    for part in range(PARTS):
        others(group, count, lambda k: row_wait(incoming.at[part, k], col_recv.at[part, k], k))

    def add(i, j):
        here = pl.ds(pl.multiple_of(j * BLK, BLK), BLK)
        for half in range(2):
            for part in range(PARTS):
                start = pl.multiple_of(i * BLK + half * HALF + part * PART, PART)
                value = root[pl.ds(start, PART), here]
                for child in range(2):
                    scale = there[(child * SLOTS + i) * SLOTS + j, 0:1, :]
                    value = value + incoming[part, half * 8 + source[child, j], child, i] * scale
                out[pl.ds(start, PART), here] = value

    edge = RP // BLK
    size = SLOTS * BLK

    @pl.loop(0, SLOTS * edge)
    def _(item):
        add(item // edge, item % edge)

    @pl.loop(0, (SLOTS - edge) * edge)
    def _(item):
        add(item % edge, edge + item // edge)

    over, under = size // count, RP // count

    def cut(ref, k, lines):
        return ref.at[pl.ds(pl.multiple_of(k * lines, lines), lines)]

    def over_first(k):
        return remote(cut(row_panel, k, over), cut(row_panel, k, over), over_cast.at[k], over_in,
                      in_row(k))

    def over_second(k):
        return remote(cut(row_panel, group, over), cut(row_panel, group, over), over_send.at[k],
                      over_recv.at[group], in_row(k))

    def down_first(k):
        return remote(cut(col_panel, k, under), cut(col_panel, k, under), down_cast.at[k],
                      down_in, in_col(k))

    def down_second(k):
        return remote(cut(col_panel, prow, under), cut(col_panel, prow, under), down_send.at[k],
                      down_recv.at[prow], in_col(k))

    def spare_first(k, body):
        @pl.when(k > 0)
        def _():
            body()

    @pl.when(prow == 0)
    def _():
        col_panel[...] = out[:RP, :]
        others(prow, count, lambda k: down_first(k).start())
        others(prow, count, lambda k: down_second(k).start())

    @pl.when(group == 0)
    def _():
        row_panel[...] = out[:, :RP]
        others(group, count, lambda k: over_first(k).start())
        others(group, count, lambda k: over_second(k).start())

    @pl.loop(0, (SLOTS - edge) * (SLOTS - edge))
    def _(item):
        add(edge + item // (SLOTS - edge), edge + item % (SLOTS - edge))

    @pl.when(group > 0)
    def _():
        over_first(group).wait_recv()
        others(group, count, lambda k: spare_first(k, lambda: over_second(k).start()))

    @pl.when(prow > 0)
    def _():
        down_first(prow).wait_recv()
        others(prow, count, lambda k: spare_first(k, lambda: down_second(k).start()))

    @pl.when(group > 0)
    def _():
        others(group, count, lambda k: row_wait(cut(row_panel, k, over), over_recv.at[k], k))

    solver = split(inverse[...])
    left = dot3(split(row_panel[...]), solver, ((1,), (1,)))

    @pl.when(prow > 0)
    def _():
        others(prow, count, lambda k: col_wait(cut(col_panel, k, under), down_recv.at[k], k))

    left_parts = split(left)
    for tile in range(size // RP):
        here = slice(tile * RP, (tile + 1) * RP)
        right = dot3(solver, split(col_panel[:, here]), ((1,), (0,)))
        trailing = out[:, here] - dot3(left_parts, split(right), ((1,), (0,)))
        upper_rows = jnp.where(prow > 0, trailing[:RP], out[:RP, here])
        lower_rows = trailing[RP:]
        if tile == 0:
            panel_rows = jnp.where(prow > 0, left[:RP], factor[...])
            upper_rows = jnp.where(group > 0, upper_rows, panel_rows)
            lower_rows = jnp.where(group > 0, lower_rows, left[RP:])
        out[:RP, here] = upper_rows
        out[RP:, here] = lower_rows

    @pl.when(group == 0)
    def _():
        others(group, count, lambda k: over_first(k).wait_send())

    @pl.when(prow == 0)
    def _():
        others(prow, count, lambda k: down_first(k).wait_send())

    others(group, count, lambda k: spare_first(k, lambda: over_second(k).wait_send()))
    others(prow, count, lambda k: spare_first(k, lambda: down_second(k).wait_send()))
    for part in range(PARTS):
        others(prow, count, lambda k: row_copy(part, k).wait_send())
        others(group, count, lambda k: col_copy(part, k).wait_send())
    others(group, count, lambda k: scatter(k).wait_send())
    others(prow, count, lambda k: across(k).wait_send())
    others(group, count, lambda k: gather(k).wait_send())


def exchange(rows, cols, lead_at, source, weight, there, outgoing, root):
    count = COUNT
    vmem = pl.BlockSpec(memory_space=pltpu.VMEM)
    smem = pl.BlockSpec(memory_space=pltpu.SMEM)
    shape = (PARTS, count, 2, SLOTS, PART, BLK)
    piece = (RP // count, RP)
    one, many = pltpu.SemaphoreType.DMA, pltpu.SemaphoreType.DMA((count,))
    pieces = pltpu.VMEM((count,) + piece, jnp.float32)
    square = pltpu.VMEM((RP, RP), jnp.float32)
    corner = pltpu.VMEM((BLK, BLK), jnp.float32)
    return pl.pallas_call(
        exchange_kernel,
        out_shape=jax.ShapeDtypeStruct(root.shape, jnp.float32),
        in_specs=[smem, smem, smem, smem, vmem, vmem, vmem, vmem],
        out_specs=vmem,
        scratch_shapes=[pltpu.VMEM(shape, jnp.float32), square, square,
                        pltpu.VMEM(shape, jnp.float32),
                        pieces, pieces, pltpu.VMEM(piece, jnp.float32), pieces, pieces,
                        corner, corner, pltpu.VMEM((root.shape[0], RP), jnp.float32),
                        pltpu.VMEM((RP, root.shape[1]), jnp.float32)]
        + [pltpu.SemaphoreType.DMA((PARTS, count))] * 4 + [many] * 6
        + [many, one, many, many] * 2
        + [pltpu.VMEM(outgoing.shape[1:], jnp.float32)] * PARTS,
        compiler_params=pltpu.CompilerParams(collective_id=3, has_side_effects=True),
    )(rows, cols, lead_at, source, weight, there, outgoing, root)


def shards(child_update, child_panel, root_front, index_map):
    leaves, rows, cols, lead_at, source, weight, there = tables(index_map)
    outgoing = spread(leaves, child_panel[0], child_update[0])
    return exchange(rows, cols, lead_at, source, weight, there, outgoing, root_front)


def solution(mesh):
    return jax.shard_map(
        shards,
        mesh=mesh,
        in_specs=(
            P("half", "prow", "pcol"),
            P("half", "prow", None),
            P("prow", ("half", "pcol")),
            P(),
        ),
        out_specs=P("prow", ("half", "pcol")),
        check_vma=False,
    )
```
